32 devices in a mesh: px: 8 (over z, x), py: 4 (over y, core).
Axes of the slice: x: 2, y: 2, z: 4, core: 2. Of those that a mesh axis runs over, the one named last changes fastest.
Arguments:
- particles: float32 [32, 2, 2, 128, 128], P(('px', 'py')), may hold values from -11 to 11
- orientation: int32 [32], P(('px', 'py')), may hold values from 0 to 7
- wedge_index: int32 [32], P(('px', 'py')), may hold values from 0 to 3
- half_set: int32 [32], P(('px', 'py')), may hold values from 0 to 1
- shell_map: int32 [2, 256, 256], P(None, ('px', 'py')), may hold values from 0 to 31, as said below
Outputs:
- half_maps: float32 [2, 2, 2, 256, 256], P(None, None, None, ('px', 'py'))
- fsc: float32 [32], replicated
The draws below stay inside these ranges and needn't reach their ends.
Inputs may be any that keep to these rules, and one draw needn't show every extreme that they name: `shell_map`: every shell number occurs in every draw.
All inputs are finite; a program needn't handle non-finite values.
Results may differ from the reference program's by a relative error of at most 0.0003.
Values sent between devices are 32-bit elements; how exact they have to be, the bound alone decides.
No kernel may reach another device: no remote copies, remote signals or barrier semaphores. Data moves between devices by JAX's collectives and lax.ppermute only.
A program may use at most 64 MiB of HBM per device.

```python
import functools
import jax
import jax.numpy as jnp
from jax import lax

N = 256
BOX = 128
NZ = 2
NSHELL = 32
PARTICLES = 32


def draw_particles(key, part):
    full_shape = (PARTICLES, 2, NZ, BOX, BOX)
    common = 0.8 * jnp.clip(jax.random.normal(jax.random.fold_in(key, 11), full_shape[1:], jnp.float32), -6.0, 6.0)
    noise = jnp.clip(jax.random.normal(jax.random.fold_in(key, 12), full_shape, jnp.float32), -6.0, 6.0)
    return common[None] + noise


def draw_shell_map(key, part):
    weights_axis = jax.random.randint(jax.random.fold_in(key, 21), (3,), 4, 10, dtype=jnp.int32)
    spectral = jnp.arange(N, dtype=jnp.int32)
    signed = jnp.where(spectral < N // 2, spectral, spectral - N)
    planes = (jnp.arange(NZ, dtype=jnp.int32) - NZ // 2) * (N // NZ)
    radius_sq = weights_axis[2] * planes[:, None, None] ** 2 + weights_axis[0] * signed[None, :, None] ** 2 + weights_axis[1] * signed[None, None, :] ** 2
    spacing = N // NSHELL
    bounds = (jnp.arange(1, NSHELL, dtype=jnp.int32) * spacing) ** 2
    return jnp.sum((radius_sq[..., None] >= bounds).astype(jnp.int32), axis=-1)


def touch_ends(result, stream_key, smallest, high):
    extent = result.shape
    place = [jax.random.randint(jax.random.fold_in(stream_key, axis), (), 0, extent[axis]) for axis in range(len(extent))]
    result = result.at[tuple(place)].set(smallest)
    longest = extent.index(max(extent))
    place[longest] = (place[longest] + 1) % extent[longest]
    return result.at[tuple(place)].set(high)


def setup_inputs(seed: int = 0) -> dict:
    arg_keys = jax.random.split(jax.random.key(seed), 6)
    return {
        "particles": draw_particles(jax.random.fold_in(arg_keys[5], 71), 0),
        "orientation": touch_ends(jax.random.randint(arg_keys[1], (PARTICLES,), 0, 8), jax.random.fold_in(arg_keys[1], 1), 0, 7).astype(jnp.int32),
        "wedge_index": touch_ends(jax.random.randint(arg_keys[2], (PARTICLES,), 0, 4), jax.random.fold_in(arg_keys[2], 1), 0, 3).astype(jnp.int32),
        "half_set": touch_ends(jax.random.randint(arg_keys[3], (PARTICLES,), 0, 2), jax.random.fold_in(arg_keys[3], 1), 0, 1).astype(jnp.int32),
        "shell_map": draw_shell_map(jax.random.fold_in(arg_keys[5], 71), 0),
    }


wedge_rise = (1, 3, 2, 3)
wedge_run = (1, 2, 1, 1)

def negate(values, dimension):
    return jnp.roll(jnp.flip(values, dimension), 1, dimension)

def quarter(values):
    return jnp.swapaxes(negate(values, -1), -1, -2)

def orient_branch(values, turns, mirror):
    for repeat in range(turns):
        values = quarter(values)
    if mirror:
        values = negate(negate(values, -3), -1)
    return values

def reference(particles, orientation, wedge_index, half_set, shell_map):
    plane_abs = jnp.abs((jnp.arange(NZ, dtype=jnp.int32) - NZ // 2) * (N // NZ))
    spectral = jnp.arange(N, dtype=jnp.int32)
    spectral_abs = jnp.minimum(spectral, N - spectral)
    rise_table = jnp.array(wedge_rise, dtype=jnp.int32)
    run_table = jnp.array(wedge_run, dtype=jnp.int32)
    branches = [functools.partial(orient_branch, turns=code % 4, mirror=code >= 4) for code in range(8)]

    def accumulate(carry, item):
        totals, cover_sum = carry
        source, turn_index, wedge_id, half_id = item
        padded = jnp.zeros((2, NZ, N, N), jnp.float32).at[:, :, :BOX, :BOX].set(source)
        padded = jnp.roll(padded, (-(BOX // 2), -(BOX // 2)), axis=(2, 3))
        spectrum = jnp.fft.fft2(padded[0] + 1j * padded[1], norm='ortho')
        covered = (plane_abs[:, None] * run_table[wedge_id] <= spectral_abs[None, :] * rise_table[wedge_id]).astype(jnp.float32)
        covered = jnp.broadcast_to(covered[:, :, None], (NZ, N, N))
        stacked = jnp.stack([jnp.real(spectrum) * covered, jnp.imag(spectrum) * covered, covered])
        turned = lax.switch(turn_index, branches, stacked)
        totals = totals.at[half_id].add(turned[:2])
        cover_sum = cover_sum.at[half_id].add(turned[2])
        return ((totals, cover_sum), None)
    start = (jnp.zeros((2, 2, NZ, N, N), jnp.float32), jnp.zeros((2, NZ, N, N), jnp.float32))
    (totals, cover_sum), unused = lax.scan(accumulate, start, (particles, orientation, wedge_index, half_set))
    average = totals / jnp.maximum(cover_sum, 1.0)[:, None]
    cross = average[0, 0] * average[1, 0] + average[0, 1] * average[1, 1]
    power_first = average[0, 0] * average[0, 0] + average[0, 1] * average[0, 1]
    power_second = average[1, 0] * average[1, 0] + average[1, 1] * average[1, 1]
    labels = shell_map.reshape(-1)
    cross_sum = jax.ops.segment_sum(cross.reshape(-1), labels, num_segments=NSHELL)
    first_sum = jax.ops.segment_sum(power_first.reshape(-1), labels, num_segments=NSHELL)
    second_sum = jax.ops.segment_sum(power_second.reshape(-1), labels, num_segments=NSHELL)
    fsc = cross_sum / (jnp.sqrt(first_sum * second_sum) + 1e-06)
    spatial = jnp.fft.ifft2(average[:, 0] + 1j * average[:, 1], norm='ortho')
    half_maps = jnp.stack([jnp.real(spatial), jnp.imag(spatial)], axis=1)
    half_maps = jnp.swapaxes(half_maps, -1, -2)
    return (half_maps, fsc)
```

```python
import functools
import math

import jax
import jax.numpy as jnp
import numpy as np
from jax import lax
from jax.experimental import pallas as pl
from jax.experimental.pallas import tpu as pltpu
from jax.sharding import PartitionSpec as P

NSHELL = 32


wedge_rise = (1, 3, 2, 3)
wedge_run = (1, 2, 1, 1)
sign_first = (1.0, -1.0, -1.0, 1.0, 1.0, -1.0, -1.0, 1.0)
sign_second = (1.0, 1.0, -1.0, -1.0, -1.0, -1.0, 1.0, 1.0)
highest = lax.Precision.HIGHEST
axes = ("px", "py")

SUBLANES = 8
LANES = 128
NWEDGE = len(wedge_rise)
NCLASS = 1 + NWEDGE
NSLOT = 2 * NCLASS
ROW_LANE = 32


def split_table(table):
    high = table.astype(jnp.bfloat16)
    low = (table - high.astype(np.float64)).astype(jnp.bfloat16)
    return high, low


def cos_sin(sources, targets, extent):
    phases = np.outer(sources, targets) % extent
    angles = phases * (2.0 * math.pi / extent)
    factor = 1.0 / math.sqrt(extent)
    return np.cos(angles) * factor, np.sin(angles) * factor


def split(values):
    high = values.astype(jnp.bfloat16)
    low = (values - high.astype(jnp.float32)).astype(jnp.bfloat16)
    return high, low


def matmul(left, right, contract=((1,), (0,))):
    return lax.dot_general(left, right, (contract, ((), ())), preferred_element_type=jnp.float32)


def matmul_split(left, right, contract=((1,), (0,))):
    return (
        matmul(left[1], right[0], contract)
        + matmul(left[0], right[1], contract)
        + matmul(left[0], right[0], contract)
    )


def pick(lookup, position):
    value = jnp.int32(lookup[0])
    for entry in range(1, len(lookup)):
        value = jnp.where(position == entry, jnp.int32(lookup[entry]), value)
    return value


def iota(shape, dimension):
    return lax.broadcasted_iota(jnp.int32, shape, dimension)


def spread_kernel(rows, turn_ref, wedge_ref, half_ref, source_ref, high_ref, low_ref, out_ref):
    planes = source_ref.shape[2]
    box_side = source_ref.shape[3]
    extent = high_ref.shape[0]
    devices = extent // rows
    stride = out_ref.shape[0] // devices
    turn = turn_ref[0]
    wedge = wedge_ref[0]
    half = half_ref[0]
    swapped = (turn & 1) == 1
    first = jnp.where(((turn + 1) & 2) == 2, -1.0, 1.0)
    second = jnp.where(((turn + 2) & 4) == 4, -1.0, 1.0)
    rise = pick(wedge_rise, wedge)
    run = pick(wedge_run, wedge)
    plane_abs = [abs(plane - planes // 2) * (extent // planes) for plane in range(planes)]

    sign = jnp.full((1, box_side), first, jnp.float32).astype(jnp.bfloat16)
    table = []
    for ref in (high_ref, low_ref):
        table.append(jnp.concatenate([ref[:, :box_side], ref[:, box_side:] * sign], axis=1))

    def operand(axis):
        parts = ([], [])
        for plane in range(planes):
            mirrored = (planes - plane) % planes
            if mirrored == plane:
                chosen = plane
            else:
                chosen = jnp.where(turn >= 4, mirrored, plane)
            real = split(source_ref[0, 0, chosen])
            imag = split(source_ref[0, 1, chosen])
            for part in range(2):
                parts[part].append(jnp.concatenate([real[part], imag[part]], axis=axis))
                parts[part].append(jnp.concatenate([imag[part], -real[part]], axis=axis))
        return [jnp.concatenate(part, axis=1 - axis) for part in parts]

    def store(product, kept):
        for plane in range(planes):
            for part in range(2):
                column = (plane * 2 + part) * box_side
                block = product[:, column : column + box_side]
                if kept is not None and plane_abs[plane] != 0:
                    block = jnp.where(plane_abs[plane] * run <= kept * rise, block, 0.0)
                for device in range(devices):
                    start = device * stride + (part * planes + plane) * rows
                    out_ref[start : start + rows, :] = block[device * rows : (device + 1) * rows]

    @pl.when(jnp.logical_not(swapped))
    def _():
        frequency = iota((extent, box_side), 0)
        store(
            matmul_split(table, operand(0)),
            jnp.minimum(frequency, extent - frequency),
        )

    @pl.when(swapped)
    def _():
        store(matmul_split(table, operand(1), ((1,), (1,))), None)

    lane = iota((devices, LANES), 1)
    slot = half * NCLASS + jnp.where(swapped, wedge + 1, 0)
    labels = jnp.where(lane == slot, 1.0, 0.0) + jnp.where(lane == slot + NSLOT, second, 0.0)
    place = lane - ROW_LANE
    frequency = iota((devices, LANES), 0) * rows + (place & (rows - 1))
    block = place // rows
    kept_plane = jnp.abs(block % planes - planes // 2) * (extent // planes)
    kept = kept_plane * run <= jnp.minimum(frequency, extent - frequency) * rise
    ours = (block // planes == half) & (place >= 0) & jnp.logical_not(swapped)
    labels = labels + jnp.where(kept & ours, 1.0, 0.0)
    out_ref[pl.ds(stride - 1, devices, stride=stride), :] = labels


def average_kernel(rows, planes, arrived_ref, shell_ref, high_ref, low_ref, out_ref):
    extent = shell_ref.shape[2]
    devices = extent // rows
    stride = arrived_ref.shape[0] // devices
    out_stride = out_ref.shape[0] // devices
    plane_abs = [abs(plane - planes // 2) * (extent // planes) for plane in range(planes)]
    labels = arrived_ref[pl.ds(stride - 1, devices, stride=stride), :]
    labels_low = labels.astype(jnp.bfloat16)

    slot_rows = 2 * NSLOT * rows
    slot_of = jnp.where(
        iota((slot_rows, LANES), 0) // rows == iota((slot_rows, LANES), 1), 1.0, 0.0
    ).astype(jnp.bfloat16)
    by_particle = matmul(slot_of, labels_low, ((1,), (1,))).astype(jnp.bfloat16)
    spread = jnp.where(
        iota((devices, extent), 1) // rows == iota((devices, extent), 0), 1.0, 0.0
    ).astype(jnp.bfloat16)
    chosen = matmul(by_particle, spread)
    same_row = (iota((slot_rows, extent), 0) & (rows - 1)) == (
        iota((slot_rows, extent), 1) & (rows - 1)
    )
    chosen = jnp.where(same_row, chosen, 0.0).astype(jnp.bfloat16)
    columns = []
    for block in range(2 * planes):
        pieces = [
            arrived_ref[device * stride + block * rows : device * stride + (block + 1) * rows, :]
            for device in range(devices)
        ]
        columns.append(jnp.concatenate(pieces, axis=0))
    stacked = split(jnp.concatenate(columns, axis=1))
    sums = matmul(chosen, stacked[1]) + matmul(chosen, stacked[0])

    class_rows = NSLOT * rows
    left = []
    for part in range(2):
        for plane in range(planes):
            plain = sums[:class_rows, (part * planes + plane) * LANES :][:, :LANES]
            other = sums[class_rows:, ((1 - part) * planes + plane) * LANES :][:, :LANES]
            left.append(jnp.concatenate([plain, other if part == 0 else -other], axis=1))
    lower = extent - LANES // 2
    forward = [
        jnp.concatenate(
            [ref[lower:, :extent], ref[: LANES // 2, :extent]]
            + [ref[lower:, extent:], ref[: LANES // 2, extent:]],
            axis=0,
        )
        for ref in (high_ref, low_ref)
    ]
    turned = matmul_split(split(jnp.concatenate(left, axis=0)), forward)

    counts = matmul(jnp.ones((rows, devices), jnp.bfloat16), labels_low)
    lane = iota((rows, LANES), 1)
    frequency = iota((1, extent), 1)
    frequency_abs = jnp.minimum(frequency, extent - frequency)
    masks = [
        [
            None
            if plane_abs[plane] == 0
            else plane_abs[plane] * wedge_run[wedge] <= frequency_abs * wedge_rise[wedge]
            for wedge in range(NWEDGE)
        ]
        for plane in range(planes)
    ]
    averages = {}
    for half in range(2):
        swapped_counts = [
            jnp.sum(
                jnp.where(lane == half * NCLASS + 1 + wedge, counts, 0.0), axis=1, keepdims=True
            )
            for wedge in range(NWEDGE)
        ]
        for plane in range(planes):
            place = ROW_LANE + (half * planes + plane) * rows
            cover = jnp.sum(
                jnp.where(lane == place + iota((rows, LANES), 0), counts, 0.0),
                axis=1,
                keepdims=True,
            )
            cover = jnp.broadcast_to(cover, (rows, extent))
            for wedge in range(NWEDGE):
                mask = masks[plane][wedge]
                if mask is None:
                    cover = cover + swapped_counts[wedge]
                else:
                    cover = cover + jnp.where(mask, swapped_counts[wedge], 0.0)
            inverse = 1.0 / jnp.maximum(cover, 1.0)
            for part in range(2):
                base = ((part * planes + plane) * NSLOT + half * NCLASS) * rows
                total = turned[base : base + rows]
                for wedge in range(NWEDGE):
                    start = base + (1 + wedge) * rows
                    term = turned[start : start + rows]
                    mask = masks[plane][wedge]
                    total = total + (term if mask is None else jnp.where(mask, term, 0.0))
                averages[half, part, plane] = total * inverse

    shell_index = iota((NSHELL, extent), 0)
    accumulated = [jnp.zeros((NSHELL, extent), jnp.float32) for _ in range(3)]
    for plane in range(planes):
        a_re, a_im = averages[0, 0, plane], averages[0, 1, plane]
        b_re, b_im = averages[1, 0, plane], averages[1, 1, plane]
        products = (
            a_re * b_re + a_im * b_im,
            a_re * a_re + a_im * a_im,
            b_re * b_re + b_im * b_im,
        )
        shells = shell_ref[plane]
        for row in range(rows):
            member = shells[row : row + 1] == shell_index
            for which in range(3):
                accumulated[which] = accumulated[which] + jnp.where(
                    member, products[which][row : row + 1], 0.0
                )
    accumulated.append(jnp.zeros((LANES - 3 * NSHELL, extent), jnp.float32))
    gathered = jnp.concatenate(accumulated, axis=0)
    pieces = []
    for _ in range(3):
        piece = gathered.astype(jnp.bfloat16)
        gathered = gathered - piece.astype(jnp.float32)
        pieces.append(piece)
    shell_sums = matmul(
        jnp.ones((SUBLANES, 3 * extent), jnp.bfloat16),
        jnp.concatenate(pieces, axis=1),
        ((1,), (1,)),
    )
    out_ref[pl.ds(out_stride - 1, devices, stride=out_stride), :] = jnp.broadcast_to(
        shell_sums[:1], (devices, LANES)
    )

    order = [(half, plane) for half in range(2) for plane in range(planes)]
    backward = jnp.concatenate(
        [averages[half, part, plane] for part in range(2) for half, plane in order], axis=0
    )
    back = matmul_split(split(backward), [high_ref[...], low_ref[...]])
    offset = len(order) * rows
    blocks = {}
    for number, (half, plane) in enumerate(order):
        real = back[number * rows : (number + 1) * rows]
        imag = back[offset + number * rows : offset + (number + 1) * rows]
        blocks[half, 0, plane] = real[:, :extent] - imag[:, extent:]
        blocks[half, 1, plane] = real[:, extent:] + imag[:, :extent]
    sequence = [
        blocks[half, part, plane]
        for half in range(2)
        for part in range(2)
        for plane in range(planes)
    ]
    lane = iota((rows, LANES), 1)
    straight = lane // (LANES // 2) == iota((rows, LANES), 0) // (rows // 2)
    group_size = LANES // rows
    for group in range(extent // LANES):
        tiles = [block[:, group * LANES : (group + 1) * LANES] for block in sequence]
        distance = 1
        while distance < len(tiles):
            shift = distance * rows
            clear = (lane & shift) == 0
            for low in range(len(tiles)):
                if low & distance:
                    continue
                high = low | distance
                a, b = tiles[low], tiles[high]
                tiles[low] = jnp.where(clear, a, pltpu.roll(b, shift, 1))
                tiles[high] = jnp.where(clear, pltpu.roll(a, LANES - shift, 1), b)
            distance *= 2
        for number, tile in enumerate(tiles):
            crossed = pltpu.roll(pltpu.roll(tile, LANES // 2, 1), rows // 2, 0)
            packed = jnp.where(straight, tile, crossed)
            for upper in range(2):
                device = group * group_size + upper * (group_size // 2) + number
                start = device * out_stride
                out_ref[start : start + rows // 2, :] = packed[
                    upper * (rows // 2) : (upper + 1) * (rows // 2)
                ]


def finish_kernel(rows, arrived_ref, high_ref, low_ref, maps_ref, fsc_ref):
    halves, parts, planes, own, extent = maps_ref.shape
    devices = extent // rows
    stride = arrived_ref.shape[0] // devices
    total = jnp.sum(
        arrived_ref[pl.ds(stride - 1, devices, stride=stride), :], axis=0, keepdims=True
    )
    cross = total[:, :NSHELL]
    power = total[:, NSHELL : 2 * NSHELL] * total[:, 2 * NSHELL : 3 * NSHELL]
    fsc_ref[...] = cross / (jnp.sqrt(power) + 1e-06)

    gathered = jnp.concatenate(
        [arrived_ref[pl.ds(row, devices, stride=stride), :] for row in range(rows // 2)], axis=0
    )
    turned = gathered.T
    left = jnp.concatenate([turned[: LANES // 2], turned[LANES // 2 :]], axis=1)
    final = matmul_split(split(left), [high_ref[...], low_ref[...]])
    for half in range(halves):
        for plane in range(planes):
            real_at = ((half * parts + 0) * planes + plane) * own
            imag_at = ((half * parts + 1) * planes + plane) * own
            real = final[real_at : real_at + own]
            imag = final[imag_at : imag_at + own]
            maps_ref[half, 0, plane] = real[:, :extent] - imag[:, extent:]
            maps_ref[half, 1, plane] = real[:, extent:] + imag[:, :extent]


def in_vmem(count):
    return [pl.BlockSpec(memory_space=pltpu.VMEM)] * count


def exchange(values, devices):
    chunks = values.reshape(devices, values.shape[0] // devices, 1, LANES)
    return lax.all_to_all(chunks, axes, 0, 0, tiled=True).reshape(values.shape)


def fits(particles, shell_map, devices):
    rows = shell_map.shape[1]
    planes = particles.shape[2]
    extent = shell_map.shape[2]
    return (
        particles.shape[0] == 1
        and rows == SUBLANES
        and rows * devices == extent
        and particles.shape[3] == LANES
        and extent % LANES == 0
        and 4 * planes * rows * 2 == LANES
        and ROW_LANE + 2 * planes * rows <= LANES
        and extent * 2 >= LANES
    )


def shards(particles, orientation, wedge_index, half_set, shell_map):
    devices = lax.axis_size("px") * lax.axis_size("py")
    if not fits(particles, shell_map, devices):
        return general(particles, orientation, wedge_index, half_set, shell_map)
    planes = particles.shape[2]
    box_side = particles.shape[3]
    rows = shell_map.shape[1]
    extent = shell_map.shape[2]
    spectral = np.arange(extent)
    smem = [pl.BlockSpec(memory_space=pltpu.SMEM)] * 3

    along_x = np.concatenate(
        cos_sin(spectral, np.arange(box_side) - box_side // 2, extent), axis=1
    )
    x_high, x_low = split_table(along_x)
    full = np.concatenate(cos_sin(spectral, spectral, extent), axis=1)
    y_high, y_low = split_table(full)
    half_rows = rows // 2
    arrival = (
        np.arange(2)[:, None, None] * half_rows
        + np.arange(half_rows)[None, :, None]
        + np.arange(devices)[None, None, :] * rows
    ).reshape(-1)
    back_high, back_low = split_table(full[arrival])

    sent = pl.pallas_call(
        functools.partial(spread_kernel, rows),
        out_shape=jax.ShapeDtypeStruct((devices * (2 * planes * rows + 1), LANES), jnp.float32),
        in_specs=smem + in_vmem(3),
        out_specs=in_vmem(1)[0],
    )(orientation, wedge_index, half_set, particles, x_high, x_low)
    arrived = exchange(sent, devices)
    middle = pl.pallas_call(
        functools.partial(average_kernel, rows, planes),
        out_shape=jax.ShapeDtypeStruct((devices * (half_rows + 1), LANES), jnp.float32),
        in_specs=in_vmem(4),
        out_specs=in_vmem(1)[0],
    )(arrived, shell_map, y_high, y_low)
    returned = exchange(middle, devices)
    half_maps, fsc = pl.pallas_call(
        functools.partial(finish_kernel, rows),
        out_shape=(
            jax.ShapeDtypeStruct((2, 2, planes, rows, extent), jnp.float32),
            jax.ShapeDtypeStruct((1, NSHELL), jnp.float32),
        ),
        in_specs=in_vmem(3),
        out_specs=tuple(in_vmem(2)),
    )(returned, back_high, back_low)
    return half_maps, fsc.reshape(NSHELL)


def select(lookup, position):
    entries = jnp.array(lookup)
    return jnp.sum(jnp.where(jnp.arange(len(lookup)) == position, entries, jnp.zeros_like(entries)))


def angle_table(sources, targets, extent):
    phases = sources[:, None] * targets[None, :] % extent
    angles = phases.astype(jnp.float32) * (2.0 * math.pi / extent)
    factor = 1.0 / math.sqrt(extent)
    return (jnp.cos(angles) * factor, jnp.sin(angles) * factor)


def coverage(plane_abs, spectral_abs, wedge_id):
    rise_value = select(wedge_rise, wedge_id)
    run_value = select(wedge_run, wedge_id)
    return (plane_abs[:, None] * run_value <= spectral_abs[None, :] * rise_value).astype(
        jnp.float32
    )


def general(particles, orientation, wedge_index, half_set, shell_map):
    planes = particles.shape[2]
    box_side = particles.shape[3]
    extent = shell_map.shape[2]
    own_rows = shell_map.shape[1]
    plane_abs = jnp.abs((jnp.arange(planes, dtype=jnp.int32) - planes // 2) * (extent // planes))
    spectral = jnp.arange(extent, dtype=jnp.int32)
    spectral_abs = jnp.minimum(spectral, extent - spectral)
    cos_fwd, sin_fwd = angle_table(
        jnp.arange(box_side, dtype=jnp.int32) - box_side // 2, spectral, extent
    )
    totals = jnp.zeros((2, 2, planes, extent, extent), jnp.float32)
    source = particles[0]
    turn_index = orientation[0]
    swapped = turn_index % 2 == 1
    source = jnp.where(turn_index >= 4, jnp.roll(jnp.flip(source, 1), 1, 1), source)
    source = jnp.where(swapped, jnp.swapaxes(source, 2, 3), source)
    sign_outer = select(sign_first, turn_index)
    sign_inner = select(sign_second, turn_index)
    along_cos = jnp.einsum("czab,bk->czak", source, cos_fwd, precision=highest)
    along_sin = jnp.einsum("czab,bk->czak", source, sin_fwd, precision=highest)
    partial_turn = jnp.stack(
        [along_cos[0] + sign_inner * along_sin[1], along_cos[1] - sign_inner * along_sin[0]]
    )
    outer_cos = jnp.einsum("czak,aj->czjk", partial_turn, cos_fwd, precision=highest)
    outer_sin = jnp.einsum("czak,aj->czjk", partial_turn, sin_fwd, precision=highest)
    spectrum = jnp.stack(
        [outer_cos[0] + sign_outer * outer_sin[1], outer_cos[1] - sign_outer * outer_sin[0]]
    )
    covered = coverage(plane_abs, spectral_abs, wedge_index[0])
    covered = jnp.where(swapped, covered[:, None, :], covered[:, :, None])
    half_id = half_set[0]
    current = lax.dynamic_index_in_dim(totals, half_id, 0, False)
    totals = lax.dynamic_update_index_in_dim(totals, current + spectrum * covered, half_id, 0)
    reduced = lax.psum_scatter(totals, ("px", "py"), scatter_dimension=3, tiled=True)
    half_hot = (half_set[:, None] == jnp.arange(2)).astype(jnp.float32)
    wedge_hot = (wedge_index[:, None] == jnp.arange(4)).astype(jnp.float32)
    parity_hot = (orientation[:, None] % 2 == jnp.arange(2)).astype(jnp.float32)
    local_counts = jnp.einsum("ph,pw,pq->hwq", half_hot, wedge_hot, parity_hot, precision=highest)
    class_totals = lax.psum(local_counts, ("px", "py"))
    row_abs = lax.dynamic_slice_in_dim(
        spectral_abs, lax.axis_index(("px", "py")) * own_rows, own_rows
    )
    row_cover = jnp.stack([coverage(plane_abs, row_abs, wedge_id) for wedge_id in range(4)])
    column_cover = jnp.stack([coverage(plane_abs, spectral_abs, wedge_id) for wedge_id in range(4)])
    by_rows = jnp.einsum("hw,wzt->hzt", class_totals[:, :, 0], row_cover, precision=highest)
    by_columns = jnp.einsum("hw,wzk->hzk", class_totals[:, :, 1], column_cover, precision=highest)
    cover = by_rows[:, :, :, None] + by_columns[:, :, None, :]
    average = reduced / jnp.maximum(cover, 1.0)[:, None]
    cross = average[0, 0] * average[1, 0] + average[0, 1] * average[1, 1]
    power_first = average[0, 0] * average[0, 0] + average[0, 1] * average[0, 1]
    power_second = average[1, 0] * average[1, 0] + average[1, 1] * average[1, 1]
    stacked = jnp.stack([cross, power_first, power_second]).reshape(3, -1)
    membership = (shell_map.reshape(-1)[:, None] == jnp.arange(NSHELL)).astype(jnp.float32)
    shell_part = jnp.dot(stacked, membership, precision=highest)
    shell_total = lax.psum(shell_part, ("px", "py"))
    fsc = shell_total[0] / (jnp.sqrt(shell_total[1] * shell_total[2]) + 1e-06)
    n_rows = lax.axis_size("px")
    n_columns = lax.axis_size("py")
    cos_y, sin_y = angle_table(spectral, spectral, extent)
    middle_cos = jnp.einsum("hcztk,kp->hczpt", average, cos_y, precision=highest)
    middle_sin = jnp.einsum("hcztk,kp->hczpt", average, sin_y, precision=highest)
    middle = jnp.stack(
        [middle_cos[:, 0] - middle_sin[:, 1], middle_sin[:, 0] + middle_cos[:, 1]], axis=1
    )
    arrived = lax.all_to_all(
        lax.all_to_all(middle, "px", split_axis=3, concat_axis=4, tiled=True),
        "py",
        split_axis=3,
        concat_axis=4,
        tiled=True,
    )
    x_slot = spectral // own_rows
    x_source = (x_slot % n_rows * n_columns + x_slot // n_rows) * own_rows + spectral % own_rows
    cos_x, sin_x = angle_table(x_source, spectral, extent)
    final_cos = jnp.einsum("hczym,mx->hczyx", arrived, cos_x, precision=highest)
    final_sin = jnp.einsum("hczym,mx->hczyx", arrived, sin_x, precision=highest)
    half_maps = jnp.stack(
        [final_cos[:, 0] - final_sin[:, 1], final_sin[:, 0] + final_cos[:, 1]], axis=1
    )
    return (half_maps, fsc)


def solution(mesh):
    placed = (
        P(("px", "py"), None, None, None, None),
        P(("px", "py")),
        P(("px", "py")),
        P(("px", "py")),
        P(None, ("px", "py"), None),
    )
    return jax.shard_map(
        shards,
        mesh=mesh,
        in_specs=placed,
        out_specs=(P(None, None, None, ("px", "py"), None), P()),
        check_vma=False,
    )
```

```python
import functools
import math

import jax
import jax.numpy as jnp
import numpy as np
from jax import lax
from jax.experimental import pallas as pl
from jax.experimental.pallas import tpu as pltpu
from jax.sharding import PartitionSpec as P

NSHELL = 32


wedge_rise = (1, 3, 2, 3)
wedge_run = (1, 2, 1, 1)
sign_first = (1.0, -1.0, -1.0, 1.0, 1.0, -1.0, -1.0, 1.0)
sign_second = (1.0, 1.0, -1.0, -1.0, -1.0, -1.0, 1.0, 1.0)
highest = lax.Precision.HIGHEST
axes = ("px", "py")

SUBLANES = 8
LANES = 128
NWEDGE = len(wedge_rise)
NCLASS = 1 + NWEDGE
NSLOT = 2 * NCLASS
ROW_LANE = 32


def split_table(table):
    high = table.astype(jnp.bfloat16)
    low = (table - high.astype(np.float64)).astype(jnp.bfloat16)
    return high, low


def cos_sin(sources, targets, extent):
    phases = np.outer(sources, targets) % extent
    angles = phases * (2.0 * math.pi / extent)
    factor = 1.0 / math.sqrt(extent)
    return np.cos(angles) * factor, np.sin(angles) * factor


def split(values):
    high = values.astype(jnp.bfloat16)
    low = (values - high.astype(jnp.float32)).astype(jnp.bfloat16)
    return high, low


def matmul(left, right, contract=((1,), (0,))):
    return lax.dot_general(left, right, (contract, ((), ())), preferred_element_type=jnp.float32)


def matmul_split(left, right, contract=((1,), (0,))):
    return (
        matmul(left[1], right[0], contract)
        + matmul(left[0], right[1], contract)
        + matmul(left[0], right[0], contract)
    )


def pick(lookup, position):
    value = jnp.int32(lookup[0])
    for entry in range(1, len(lookup)):
        value = jnp.where(position == entry, jnp.int32(lookup[entry]), value)
    return value


def iota(shape, dimension):
    return lax.broadcasted_iota(jnp.int32, shape, dimension)


def spread_kernel(
    rows, turn_ref, wedge_ref, half_ref, source_hbm, high_hbm, low_hbm, out_ref, *scratch
):
    source_ref, high_ref, low_ref, arrivals = scratch
    pairs = (
        (source_hbm, source_ref),
        (high_hbm, high_ref),
        (low_hbm, low_ref),
    )
    copies = [
        pltpu.make_async_copy(there, here, arrivals.at[number])
        for number, (there, here) in enumerate(pairs)
    ]
    for copy in copies:
        copy.start()
    for copy in copies:
        copy.wait()
    planes = source_ref.shape[2]
    box_side = source_ref.shape[3]
    extent = high_ref.shape[0]
    devices = extent // rows
    stride = out_ref.shape[0] // devices
    turn = turn_ref[0]
    wedge = wedge_ref[0]
    half = half_ref[0]
    swapped = (turn & 1) == 1
    first = jnp.where(((turn + 1) & 2) == 2, -1.0, 1.0)
    second = jnp.where(((turn + 2) & 4) == 4, -1.0, 1.0)
    rise = pick(wedge_rise, wedge)
    run = pick(wedge_run, wedge)
    plane_abs = [abs(plane - planes // 2) * (extent // planes) for plane in range(planes)]

    sign = jnp.full((1, box_side), first, jnp.float32).astype(jnp.bfloat16)
    table = []
    for ref in (high_ref, low_ref):
        table.append(jnp.concatenate([ref[:, :box_side], ref[:, box_side:] * sign], axis=1))

    def operand(axis):
        parts = ([], [])
        for plane in range(planes):
            mirrored = (planes - plane) % planes
            if mirrored == plane:
                chosen = plane
            else:
                chosen = jnp.where(turn >= 4, mirrored, plane)
            real = split(source_ref[0, 0, chosen])
            imag = split(source_ref[0, 1, chosen])
            for part in range(2):
                parts[part].append(jnp.concatenate([real[part], imag[part]], axis=axis))
                parts[part].append(jnp.concatenate([imag[part], -real[part]], axis=axis))
        return [jnp.concatenate(part, axis=1 - axis) for part in parts]

    def store(product, kept):
        for plane in range(planes):
            for part in range(2):
                column = (plane * 2 + part) * box_side
                block = product[:, column : column + box_side]
                if kept is not None and plane_abs[plane] != 0:
                    block = jnp.where(plane_abs[plane] * run <= kept * rise, block, 0.0)
                for device in range(devices):
                    start = device * stride + (part * planes + plane) * rows
                    out_ref[start : start + rows, :] = block[device * rows : (device + 1) * rows]

    @pl.when(jnp.logical_not(swapped))
    def _():
        frequency = iota((extent, box_side), 0)
        store(
            matmul_split(table, operand(0)),
            jnp.minimum(frequency, extent - frequency),
        )

    @pl.when(swapped)
    def _():
        store(matmul_split(table, operand(1), ((1,), (1,))), None)

    lane = iota((devices, LANES), 1)
    slot = half * NCLASS + jnp.where(swapped, wedge + 1, 0)
    labels = jnp.where(lane == slot, 1.0, 0.0) + jnp.where(lane == slot + NSLOT, second, 0.0)
    place = lane - ROW_LANE
    frequency = iota((devices, LANES), 0) * rows + (place & (rows - 1))
    block = place // rows
    kept_plane = jnp.abs(block % planes - planes // 2) * (extent // planes)
    kept = kept_plane * run <= jnp.minimum(frequency, extent - frequency) * rise
    ours = (block // planes == half) & (place >= 0) & jnp.logical_not(swapped)
    labels = labels + jnp.where(kept & ours, 1.0, 0.0)
    out_ref[pl.ds(stride - 1, devices, stride=stride), :] = labels


def average_kernel(rows, planes, arrived_ref, shell_ref, high_ref, low_ref, out_ref):
    extent = shell_ref.shape[2]
    devices = extent // rows
    stride = arrived_ref.shape[0] // devices
    out_stride = out_ref.shape[0] // devices
    plane_abs = [abs(plane - planes // 2) * (extent // planes) for plane in range(planes)]
    labels = arrived_ref[pl.ds(stride - 1, devices, stride=stride), :]
    labels_low = labels.astype(jnp.bfloat16)

    slot_rows = 2 * NSLOT * rows
    slot_of = jnp.where(
        iota((slot_rows, LANES), 0) // rows == iota((slot_rows, LANES), 1), 1.0, 0.0
    ).astype(jnp.bfloat16)
    by_particle = matmul(slot_of, labels_low, ((1,), (1,))).astype(jnp.bfloat16)
    spread = jnp.where(
        iota((devices, extent), 1) // rows == iota((devices, extent), 0), 1.0, 0.0
    ).astype(jnp.bfloat16)
    chosen = matmul(by_particle, spread)
    same_row = (iota((slot_rows, extent), 0) & (rows - 1)) == (
        iota((slot_rows, extent), 1) & (rows - 1)
    )
    chosen = jnp.where(same_row, chosen, 0.0).astype(jnp.bfloat16)
    columns = []
    for block in range(2 * planes):
        pieces = [
            arrived_ref[device * stride + block * rows : device * stride + (block + 1) * rows, :]
            for device in range(devices)
        ]
        columns.append(jnp.concatenate(pieces, axis=0))
    stacked = split(jnp.concatenate(columns, axis=1))
    sums = matmul(chosen, stacked[1]) + matmul(chosen, stacked[0])

    class_rows = NSLOT * rows
    left = []
    for part in range(2):
        for plane in range(planes):
            plain = sums[:class_rows, (part * planes + plane) * LANES :][:, :LANES]
            other = sums[class_rows:, ((1 - part) * planes + plane) * LANES :][:, :LANES]
            left.append(jnp.concatenate([plain, other if part == 0 else -other], axis=1))
    lower = extent - LANES // 2
    forward = [
        jnp.concatenate(
            [ref[lower:, :extent], ref[: LANES // 2, :extent]]
            + [ref[lower:, extent:], ref[: LANES // 2, extent:]],
            axis=0,
        )
        for ref in (high_ref, low_ref)
    ]
    turned = matmul_split(split(jnp.concatenate(left, axis=0)), forward)

    counts = matmul(jnp.ones((rows, devices), jnp.bfloat16), labels_low)
    lane = iota((rows, LANES), 1)
    frequency = iota((1, extent), 1)
    frequency_abs = jnp.minimum(frequency, extent - frequency)
    masks = [
        [
            None
            if plane_abs[plane] == 0
            else plane_abs[plane] * wedge_run[wedge] <= frequency_abs * wedge_rise[wedge]
            for wedge in range(NWEDGE)
        ]
        for plane in range(planes)
    ]
    averages = {}
    for half in range(2):
        swapped_counts = [
            jnp.sum(
                jnp.where(lane == half * NCLASS + 1 + wedge, counts, 0.0), axis=1, keepdims=True
            )
            for wedge in range(NWEDGE)
        ]
        for plane in range(planes):
            place = ROW_LANE + (half * planes + plane) * rows
            cover = jnp.sum(
                jnp.where(lane == place + iota((rows, LANES), 0), counts, 0.0),
                axis=1,
                keepdims=True,
            )
            cover = jnp.broadcast_to(cover, (rows, extent))
            for wedge in range(NWEDGE):
                mask = masks[plane][wedge]
                if mask is None:
                    cover = cover + swapped_counts[wedge]
                else:
                    cover = cover + jnp.where(mask, swapped_counts[wedge], 0.0)
            inverse = 1.0 / jnp.maximum(cover, 1.0)
            for part in range(2):
                base = ((part * planes + plane) * NSLOT + half * NCLASS) * rows
                total = turned[base : base + rows]
                for wedge in range(NWEDGE):
                    start = base + (1 + wedge) * rows
                    term = turned[start : start + rows]
                    mask = masks[plane][wedge]
                    total = total + (term if mask is None else jnp.where(mask, term, 0.0))
                averages[half, part, plane] = total * inverse

    shell_index = iota((NSHELL, extent), 0)
    accumulated = [jnp.zeros((NSHELL, extent), jnp.float32) for _ in range(3)]
    for plane in range(planes):
        a_re, a_im = averages[0, 0, plane], averages[0, 1, plane]
        b_re, b_im = averages[1, 0, plane], averages[1, 1, plane]
        products = (
            a_re * b_re + a_im * b_im,
            a_re * a_re + a_im * a_im,
            b_re * b_re + b_im * b_im,
        )
        shells = shell_ref[plane]
        for row in range(rows):
            member = shells[row : row + 1] == shell_index
            for which in range(3):
                accumulated[which] = accumulated[which] + jnp.where(
                    member, products[which][row : row + 1], 0.0
                )
    accumulated.append(jnp.zeros((LANES - 3 * NSHELL, extent), jnp.float32))
    gathered = jnp.concatenate(accumulated, axis=0)
    pieces = []
    for _ in range(3):
        piece = gathered.astype(jnp.bfloat16)
        gathered = gathered - piece.astype(jnp.float32)
        pieces.append(piece)
    shell_sums = matmul(
        jnp.ones((SUBLANES, 3 * extent), jnp.bfloat16),
        jnp.concatenate(pieces, axis=1),
        ((1,), (1,)),
    )
    out_ref[pl.ds(out_stride - 1, devices, stride=out_stride), :] = jnp.broadcast_to(
        shell_sums[:1], (devices, LANES)
    )

    order = [(half, plane) for half in range(2) for plane in range(planes)]
    backward = jnp.concatenate(
        [averages[half, part, plane] for part in range(2) for half, plane in order], axis=0
    )
    back = matmul_split(split(backward), [high_ref[...], low_ref[...]])
    offset = len(order) * rows
    blocks = {}
    for number, (half, plane) in enumerate(order):
        real = back[number * rows : (number + 1) * rows]
        imag = back[offset + number * rows : offset + (number + 1) * rows]
        blocks[half, 0, plane] = real[:, :extent] - imag[:, extent:]
        blocks[half, 1, plane] = real[:, extent:] + imag[:, :extent]
    sequence = [
        blocks[half, part, plane]
        for half in range(2)
        for part in range(2)
        for plane in range(planes)
    ]
    lane = iota((rows, LANES), 1)
    straight = lane // (LANES // 2) == iota((rows, LANES), 0) // (rows // 2)
    group_size = LANES // rows
    for group in range(extent // LANES):
        tiles = [block[:, group * LANES : (group + 1) * LANES] for block in sequence]
        distance = 1
        while distance < len(tiles):
            shift = distance * rows
            clear = (lane & shift) == 0
            for low in range(len(tiles)):
                if low & distance:
                    continue
                high = low | distance
                a, b = tiles[low], tiles[high]
                tiles[low] = jnp.where(clear, a, pltpu.roll(b, shift, 1))
                tiles[high] = jnp.where(clear, pltpu.roll(a, LANES - shift, 1), b)
            distance *= 2
        for number, tile in enumerate(tiles):
            crossed = pltpu.roll(pltpu.roll(tile, LANES // 2, 1), rows // 2, 0)
            packed = jnp.where(straight, tile, crossed)
            for upper in range(2):
                device = group * group_size + upper * (group_size // 2) + number
                start = device * out_stride
                out_ref[start : start + rows // 2, :] = packed[
                    upper * (rows // 2) : (upper + 1) * (rows // 2)
                ]


def finish_kernel(rows, arrived_ref, high_ref, low_ref, maps_ref, fsc_ref):
    halves, parts, planes, own, extent = maps_ref.shape
    devices = extent // rows
    stride = arrived_ref.shape[0] // devices
    total = jnp.sum(
        arrived_ref[pl.ds(stride - 1, devices, stride=stride), :], axis=0, keepdims=True
    )
    cross = total[:, :NSHELL]
    power = total[:, NSHELL : 2 * NSHELL] * total[:, 2 * NSHELL : 3 * NSHELL]
    fsc_ref[...] = cross / (jnp.sqrt(power) + 1e-06)

    gathered = jnp.concatenate(
        [arrived_ref[pl.ds(row, devices, stride=stride), :] for row in range(rows // 2)], axis=0
    )
    turned = gathered.T
    left = jnp.concatenate([turned[: LANES // 2], turned[LANES // 2 :]], axis=1)
    final = matmul_split(split(left), [high_ref[...], low_ref[...]])
    for half in range(halves):
        for plane in range(planes):
            real_at = ((half * parts + 0) * planes + plane) * own
            imag_at = ((half * parts + 1) * planes + plane) * own
            real = final[real_at : real_at + own]
            imag = final[imag_at : imag_at + own]
            maps_ref[half, 0, plane] = real[:, :extent] - imag[:, extent:]
            maps_ref[half, 1, plane] = real[:, extent:] + imag[:, :extent]


small_grant = pltpu.CompilerParams(vmem_limit_bytes=16 * 1024 * 1024)


def in_vmem(count):
    return [pl.BlockSpec(memory_space=pltpu.VMEM)] * count


def exchange(values, devices):
    chunks = values.reshape(devices, values.shape[0] // devices, 1, LANES)
    return lax.all_to_all(chunks, axes, 0, 0, tiled=True).reshape(values.shape)


def fits(particles, shell_map, devices):
    rows = shell_map.shape[1]
    planes = particles.shape[2]
    extent = shell_map.shape[2]
    return (
        particles.shape[0] == 1
        and rows == SUBLANES
        and rows * devices == extent
        and particles.shape[3] == LANES
        and extent % LANES == 0
        and 4 * planes * rows * 2 == LANES
        and ROW_LANE + 2 * planes * rows <= LANES
        and extent * 2 >= LANES
    )


def shards(particles, orientation, wedge_index, half_set, shell_map):
    devices = lax.axis_size("px") * lax.axis_size("py")
    if not fits(particles, shell_map, devices):
        return general(particles, orientation, wedge_index, half_set, shell_map)
    planes = particles.shape[2]
    box_side = particles.shape[3]
    rows = shell_map.shape[1]
    extent = shell_map.shape[2]
    spectral = np.arange(extent)

    along_x = np.concatenate(
        cos_sin(spectral, np.arange(box_side) - box_side // 2, extent), axis=1
    )
    x_high, x_low = split_table(along_x)
    full = np.concatenate(cos_sin(spectral, spectral, extent), axis=1)
    y_high, y_low = split_table(full)
    half_rows = rows // 2
    arrival = (
        np.arange(2)[:, None, None] * half_rows
        + np.arange(half_rows)[None, :, None]
        + np.arange(devices)[None, None, :] * rows
    ).reshape(-1)
    back_high, back_low = split_table(full[arrival])

    sent = pl.pallas_call(
        functools.partial(spread_kernel, rows),
        out_shape=jax.ShapeDtypeStruct((devices * (2 * planes * rows + 1), LANES), jnp.float32),
        in_specs=[pl.BlockSpec(memory_space=pltpu.SMEM)] * 3
        + [pl.BlockSpec(memory_space=pltpu.HBM)] * 3,
        out_specs=in_vmem(1)[0],
        scratch_shapes=[
            pltpu.VMEM(particles.shape, jnp.float32),
            pltpu.VMEM(x_high.shape, jnp.bfloat16),
            pltpu.VMEM(x_low.shape, jnp.bfloat16),
            pltpu.SemaphoreType.DMA((3,)),
        ],
        compiler_params=small_grant,
    )(orientation, wedge_index, half_set, pltpu.with_memory_space_constraint(particles, pltpu.HBM), pltpu.with_memory_space_constraint(jnp.asarray(x_high), pltpu.HBM), pltpu.with_memory_space_constraint(jnp.asarray(x_low), pltpu.HBM))
    arrived = exchange(sent, devices)
    middle = pl.pallas_call(
        functools.partial(average_kernel, rows, planes),
        out_shape=jax.ShapeDtypeStruct((devices * (half_rows + 1), LANES), jnp.float32),
        in_specs=in_vmem(4),
        out_specs=in_vmem(1)[0],
        compiler_params=small_grant,
    )(arrived, shell_map, y_high, y_low)
    returned = exchange(middle, devices)
    half_maps, fsc = pl.pallas_call(
        functools.partial(finish_kernel, rows),
        out_shape=(
            jax.ShapeDtypeStruct((2, 2, planes, rows, extent), jnp.float32),
            jax.ShapeDtypeStruct((1, NSHELL), jnp.float32),
        ),
        in_specs=in_vmem(3),
        out_specs=tuple(in_vmem(2)),
        compiler_params=small_grant,
    )(returned, back_high, back_low)
    return half_maps, fsc.reshape(NSHELL)


def select(lookup, position):
    entries = jnp.array(lookup)
    return jnp.sum(jnp.where(jnp.arange(len(lookup)) == position, entries, jnp.zeros_like(entries)))


def angle_table(sources, targets, extent):
    phases = sources[:, None] * targets[None, :] % extent
    angles = phases.astype(jnp.float32) * (2.0 * math.pi / extent)
    factor = 1.0 / math.sqrt(extent)
    return (jnp.cos(angles) * factor, jnp.sin(angles) * factor)


def coverage(plane_abs, spectral_abs, wedge_id):
    rise_value = select(wedge_rise, wedge_id)
    run_value = select(wedge_run, wedge_id)
    return (plane_abs[:, None] * run_value <= spectral_abs[None, :] * rise_value).astype(
        jnp.float32
    )


def general(particles, orientation, wedge_index, half_set, shell_map):
    planes = particles.shape[2]
    box_side = particles.shape[3]
    extent = shell_map.shape[2]
    own_rows = shell_map.shape[1]
    plane_abs = jnp.abs((jnp.arange(planes, dtype=jnp.int32) - planes // 2) * (extent // planes))
    spectral = jnp.arange(extent, dtype=jnp.int32)
    spectral_abs = jnp.minimum(spectral, extent - spectral)
    cos_fwd, sin_fwd = angle_table(
        jnp.arange(box_side, dtype=jnp.int32) - box_side // 2, spectral, extent
    )
    totals = jnp.zeros((2, 2, planes, extent, extent), jnp.float32)
    source = particles[0]
    turn_index = orientation[0]
    swapped = turn_index % 2 == 1
    source = jnp.where(turn_index >= 4, jnp.roll(jnp.flip(source, 1), 1, 1), source)
    source = jnp.where(swapped, jnp.swapaxes(source, 2, 3), source)
    sign_outer = select(sign_first, turn_index)
    sign_inner = select(sign_second, turn_index)
    along_cos = jnp.einsum("czab,bk->czak", source, cos_fwd, precision=highest)
    along_sin = jnp.einsum("czab,bk->czak", source, sin_fwd, precision=highest)
    partial_turn = jnp.stack(
        [along_cos[0] + sign_inner * along_sin[1], along_cos[1] - sign_inner * along_sin[0]]
    )
    outer_cos = jnp.einsum("czak,aj->czjk", partial_turn, cos_fwd, precision=highest)
    outer_sin = jnp.einsum("czak,aj->czjk", partial_turn, sin_fwd, precision=highest)
    spectrum = jnp.stack(
        [outer_cos[0] + sign_outer * outer_sin[1], outer_cos[1] - sign_outer * outer_sin[0]]
    )
    covered = coverage(plane_abs, spectral_abs, wedge_index[0])
    covered = jnp.where(swapped, covered[:, None, :], covered[:, :, None])
    half_id = half_set[0]
    current = lax.dynamic_index_in_dim(totals, half_id, 0, False)
    totals = lax.dynamic_update_index_in_dim(totals, current + spectrum * covered, half_id, 0)
    reduced = lax.psum_scatter(totals, ("px", "py"), scatter_dimension=3, tiled=True)
    half_hot = (half_set[:, None] == jnp.arange(2)).astype(jnp.float32)
    wedge_hot = (wedge_index[:, None] == jnp.arange(4)).astype(jnp.float32)
    parity_hot = (orientation[:, None] % 2 == jnp.arange(2)).astype(jnp.float32)
    local_counts = jnp.einsum("ph,pw,pq->hwq", half_hot, wedge_hot, parity_hot, precision=highest)
    class_totals = lax.psum(local_counts, ("px", "py"))
    row_abs = lax.dynamic_slice_in_dim(
        spectral_abs, lax.axis_index(("px", "py")) * own_rows, own_rows
    )
    row_cover = jnp.stack([coverage(plane_abs, row_abs, wedge_id) for wedge_id in range(4)])
    column_cover = jnp.stack([coverage(plane_abs, spectral_abs, wedge_id) for wedge_id in range(4)])
    by_rows = jnp.einsum("hw,wzt->hzt", class_totals[:, :, 0], row_cover, precision=highest)
    by_columns = jnp.einsum("hw,wzk->hzk", class_totals[:, :, 1], column_cover, precision=highest)
    cover = by_rows[:, :, :, None] + by_columns[:, :, None, :]
    average = reduced / jnp.maximum(cover, 1.0)[:, None]
    cross = average[0, 0] * average[1, 0] + average[0, 1] * average[1, 1]
    power_first = average[0, 0] * average[0, 0] + average[0, 1] * average[0, 1]
    power_second = average[1, 0] * average[1, 0] + average[1, 1] * average[1, 1]
    stacked = jnp.stack([cross, power_first, power_second]).reshape(3, -1)
    membership = (shell_map.reshape(-1)[:, None] == jnp.arange(NSHELL)).astype(jnp.float32)
    shell_part = jnp.dot(stacked, membership, precision=highest)
    shell_total = lax.psum(shell_part, ("px", "py"))
    fsc = shell_total[0] / (jnp.sqrt(shell_total[1] * shell_total[2]) + 1e-06)
    n_rows = lax.axis_size("px")
    n_columns = lax.axis_size("py")
    cos_y, sin_y = angle_table(spectral, spectral, extent)
    middle_cos = jnp.einsum("hcztk,kp->hczpt", average, cos_y, precision=highest)
    middle_sin = jnp.einsum("hcztk,kp->hczpt", average, sin_y, precision=highest)
    middle = jnp.stack(
        [middle_cos[:, 0] - middle_sin[:, 1], middle_sin[:, 0] + middle_cos[:, 1]], axis=1
    )
    arrived = lax.all_to_all(
        lax.all_to_all(middle, "px", split_axis=3, concat_axis=4, tiled=True),
        "py",
        split_axis=3,
        concat_axis=4,
        tiled=True,
    )
    x_slot = spectral // own_rows
    x_source = (x_slot % n_rows * n_columns + x_slot // n_rows) * own_rows + spectral % own_rows
    cos_x, sin_x = angle_table(x_source, spectral, extent)
    final_cos = jnp.einsum("hczym,mx->hczyx", arrived, cos_x, precision=highest)
    final_sin = jnp.einsum("hczym,mx->hczyx", arrived, sin_x, precision=highest)
    half_maps = jnp.stack(
        [final_cos[:, 0] - final_sin[:, 1], final_sin[:, 0] + final_cos[:, 1]], axis=1
    )
    return (half_maps, fsc)


def solution(mesh):
    placed = (
        P(("px", "py"), None, None, None, None),
        P(("px", "py")),
        P(("px", "py")),
        P(("px", "py")),
        P(None, ("px", "py"), None),
    )
    return jax.shard_map(
        shards,
        mesh=mesh,
        in_specs=placed,
        out_specs=(P(None, None, None, ("px", "py"), None), P()),
        check_vma=False,
    )
```

```python
import functools
import math

import jax
import jax.numpy as jnp
import numpy as np
from jax import lax
from jax.experimental import pallas as pl
from jax.experimental.pallas import tpu as pltpu
from jax.sharding import PartitionSpec as P

NSHELL = 32


wedge_rise = (1, 3, 2, 3)
wedge_run = (1, 2, 1, 1)
sign_first = (1.0, -1.0, -1.0, 1.0, 1.0, -1.0, -1.0, 1.0)
sign_second = (1.0, 1.0, -1.0, -1.0, -1.0, -1.0, 1.0, 1.0)
highest = lax.Precision.HIGHEST
axes = ("px", "py")

SUBLANES = 8
LANES = 128
NWEDGE = len(wedge_rise)
NCLASS = 1 + NWEDGE
NSLOT = 2 * NCLASS
HALF_LANE = 2 * NSLOT
ROW_LANE = 32


def split_table(table):
    high = table.astype(jnp.bfloat16)
    low = (table - high.astype(np.float64)).astype(jnp.bfloat16)
    return high, low


def cos_sin(sources, targets, extent):
    phases = np.outer(sources, targets) % extent
    angles = phases * (2.0 * math.pi / extent)
    factor = 1.0 / math.sqrt(extent)
    return np.cos(angles) * factor, np.sin(angles) * factor


def split(values):
    high = values.astype(jnp.bfloat16)
    low = (values - high.astype(jnp.float32)).astype(jnp.bfloat16)
    return high, low


def matmul(left, right, contract=((1,), (0,))):
    return lax.dot_general(left, right, (contract, ((), ())), preferred_element_type=jnp.float32)


def matmul_split(left, right, contract=((1,), (0,))):
    return (
        matmul(left[1], right[0], contract)
        + matmul(left[0], right[1], contract)
        + matmul(left[0], right[0], contract)
    )


def matmul_rows(left, right):
    count = left[0].shape[0]
    both = matmul(jnp.concatenate(left, axis=0), right[0])
    return both[:count] + (both[count:] + matmul(left[0], right[1]))


def pick(lookup, position):
    value = jnp.int32(lookup[0])
    for entry in range(1, len(lookup)):
        value = jnp.where(position == entry, jnp.int32(lookup[entry]), value)
    return value


def iota(shape, dimension):
    return lax.broadcasted_iota(jnp.int32, shape, dimension)


def label_kernel(rows, planes, extent, turn_ref, wedge_ref, half_ref, label_ref):
    devices = extent // rows
    turn = turn_ref[0]
    wedge = wedge_ref[0]
    half = half_ref[0]
    swapped = (turn & 1) == 1
    second = jnp.where(((turn + 2) & 4) == 4, -1.0, 1.0)
    rise = pick(wedge_rise, wedge)
    run = pick(wedge_run, wedge)
    lane = iota((devices, LANES), 1)
    slot = half * NCLASS + jnp.where(swapped, wedge + 1, 0)
    ones = (lane == slot) | (lane == HALF_LANE + half)
    signs = (lane == NSLOT + slot) | (lane == HALF_LANE + 2 + half)
    labels = jnp.where(ones, 1.0, jnp.where(signs, second, 0.0))
    place = lane - ROW_LANE
    frequency = iota((devices, LANES), 0) * rows + (place & (rows - 1))
    block = place // rows
    kept_plane = jnp.abs(block % planes - planes // 2) * (extent // planes)
    kept = kept_plane * run <= jnp.minimum(frequency, extent - frequency) * rise
    ours = (block // planes == half) & (place >= 0) & jnp.logical_not(swapped)
    labels = labels + jnp.where(kept & ours, 1.0, 0.0)
    label_ref[...] = labels


def spread_kernel(rows, turn_ref, wedge_ref, source_ref, table_ref, label_ref, out_ref):
    planes = source_ref.shape[2]
    box_side = source_ref.shape[3]
    extent = table_ref.shape[0]
    devices = extent // rows
    stride = out_ref.shape[0] // devices
    turn = turn_ref[0]
    wedge = wedge_ref[0]
    swapped = (turn & 1) == 1
    first = jnp.where(((turn + 1) & 2) == 2, -1.0, 1.0)
    rise = pick(wedge_rise, wedge)
    run = pick(wedge_run, wedge)
    plane_abs = [abs(plane - planes // 2) * (extent // planes) for plane in range(planes)]

    sign = jnp.full((1, box_side), first, jnp.float32).astype(jnp.bfloat16)
    table = []
    for start in (0, 2 * box_side):
        cosine = table_ref[:, start : start + box_side]
        sine = table_ref[:, start + box_side : start + 2 * box_side]
        table.append(jnp.concatenate([cosine, sine * sign], axis=1))

    def operand(axis):
        parts = ([], [])
        for plane in range(planes):
            mirrored = (planes - plane) % planes
            if mirrored == plane:
                chosen = plane
            else:
                chosen = jnp.where(turn >= 4, mirrored, plane)
            real = split(source_ref[0, 0, chosen])
            imag = split(source_ref[0, 1, chosen])
            for part in range(2):
                parts[part].append(jnp.concatenate([real[part], imag[part]], axis=axis))
                parts[part].append(jnp.concatenate([imag[part], -real[part]], axis=axis))
        return [jnp.concatenate(part, axis=1 - axis) for part in parts]

    def store(product, kept):
        for plane in range(planes):
            for part in range(2):
                column = (plane * 2 + part) * box_side
                block = product[:, column : column + box_side]
                if kept is not None and plane_abs[plane] != 0:
                    block = jnp.where(plane_abs[plane] * run <= kept * rise, block, 0.0)
                for device in range(devices):
                    start = device * stride + (part * planes + plane) * rows
                    out_ref[start : start + rows, :] = block[device * rows : (device + 1) * rows]

    @pl.when(jnp.logical_not(swapped))
    def _():
        frequency = iota((extent, box_side), 0)
        store(
            matmul_split(table, operand(0)),
            jnp.minimum(frequency, extent - frequency),
        )

    @pl.when(swapped)
    def _():
        store(matmul_split(table, operand(1), ((1,), (1,))), None)

    out_ref[pl.ds(stride - 1, devices, stride=stride), :] = label_ref[...]


def fill_flags(rows, shell_ref, member_ref, spread_ref, block_ref):
    planes, _, extent = shell_ref.shape
    shell_index = iota((NSHELL, extent), 0)
    for plane in range(planes):
        shells = shell_ref[plane]
        for row in range(rows):
            start = (plane * rows + row) * NSHELL
            member = shells[row : row + 1] == shell_index
            member_ref[start : start + NSHELL, :] = jnp.where(member, 1.0, 0.0).astype(
                jnp.bfloat16
            )

    def flag(ref, condition):
        ref[...] = jnp.where(condition, 1.0, 0.0).astype(ref.dtype)

    flag(spread_ref, iota(spread_ref.shape, 1) // rows == iota(spread_ref.shape, 0))
    flag(
        block_ref,
        iota(block_ref.shape, 0) % (planes * rows) == iota(block_ref.shape, 1) // NSHELL,
    )


def average_kernel(
    rows,
    planes,
    arrived_ref,
    shell_ref,
    high_ref,
    low_ref,
    out_ref,
    member_ref,
    spread_ref,
    block_ref,
):
    extent = high_ref.shape[0]
    fill_flags(rows, shell_ref, member_ref, spread_ref, block_ref)
    devices = extent // rows
    stride = arrived_ref.shape[0] // devices
    out_stride = out_ref.shape[0] // devices
    plane_abs = [abs(plane - planes // 2) * (extent // planes) for plane in range(planes)]
    labels = arrived_ref[pl.ds(stride - 1, devices, stride=stride), :]
    labels_low = labels.astype(jnp.bfloat16)

    slots = HALF_LANE + 4
    by_slot = matmul(labels.T[:ROW_LANE].astype(jnp.bfloat16), spread_ref[...])
    same_row = iota((rows, extent), 0) == (iota((rows, extent), 1) & (rows - 1))
    chosen = jnp.concatenate(
        [jnp.where(same_row, by_slot[slot : slot + 1], 0.0) for slot in range(slots)], axis=0
    ).astype(jnp.bfloat16)
    left = []
    base = {}
    height = 0
    for plane in range(planes):
        columns = []
        for part in range(2):
            block = part * planes + plane
            pieces = [
                arrived_ref[device * stride + block * rows : device * stride + (block + 1) * rows]
                for device in range(devices)
            ]
            columns.append(jnp.concatenate(pieces, axis=0))
        stacked = split(jnp.concatenate(columns, axis=1))
        if plane_abs[plane] == 0:
            own = chosen[HALF_LANE * rows : (HALF_LANE + 4) * rows]
        else:
            own = chosen[: 2 * NSLOT * rows]
        sums = matmul(own, stacked[1]) + matmul(own, stacked[0])
        count = own.shape[0] // 2
        plain, signed = sums[:count], sums[count:]
        left.append(jnp.concatenate([plain[:, :LANES], signed[:, LANES:]], axis=1))
        left.append(jnp.concatenate([plain[:, LANES:], -signed[:, :LANES]], axis=1))
        base[0, plane] = height
        base[1, plane] = height + count
        height += 2 * count
    lower = extent - LANES // 2
    forward = [
        jnp.concatenate(
            [ref[lower:, :extent], ref[: LANES // 2, :extent]]
            + [ref[lower:, extent:], ref[: LANES // 2, extent:]],
            axis=0,
        )
        for ref in (high_ref, low_ref)
    ]
    turned = matmul_rows(split(jnp.concatenate(left, axis=0)), forward)

    counts = matmul(jnp.ones((rows, devices), jnp.bfloat16), labels_low)
    lane = iota((rows, LANES), 1)
    frequency = iota((1, extent), 1)
    frequency_abs = jnp.minimum(frequency, extent - frequency)
    masks = [
        [
            None
            if plane_abs[plane] == 0
            else plane_abs[plane] * wedge_run[wedge] <= frequency_abs * wedge_rise[wedge]
            for wedge in range(NWEDGE)
        ]
        for plane in range(planes)
    ]
    averages = {}
    for half in range(2):
        swapped_counts = [
            jnp.sum(
                jnp.where(lane == half * NCLASS + 1 + wedge, counts, 0.0), axis=1, keepdims=True
            )
            for wedge in range(NWEDGE)
        ]
        for plane in range(planes):
            place = ROW_LANE + (half * planes + plane) * rows
            cover = jnp.sum(
                jnp.where(lane == place + iota((rows, LANES), 0), counts, 0.0),
                axis=1,
                keepdims=True,
            )
            cover = jnp.broadcast_to(cover, (rows, extent))
            for wedge in range(NWEDGE):
                mask = masks[plane][wedge]
                if mask is None:
                    cover = cover + swapped_counts[wedge]
                else:
                    cover = cover + jnp.where(mask, swapped_counts[wedge], 0.0)
            inverse = 1.0 / jnp.maximum(cover, 1.0)
            for part in range(2):
                start = base[part, plane]
                if plane_abs[plane] == 0:
                    start += half * rows
                    total = turned[start : start + rows]
                else:
                    start += half * NCLASS * rows
                    total = turned[start : start + rows]
                    for wedge in range(NWEDGE):
                        start += rows
                        term = turned[start : start + rows]
                        total = total + jnp.where(masks[plane][wedge], term, 0.0)
                averages[half, part, plane] = total * inverse

    order = [(half, plane) for half in range(2) for plane in range(planes)]
    backward = jnp.concatenate(
        [averages[half, part, plane] for part in range(2) for half, plane in order], axis=0
    )
    back = matmul_rows(split(backward), [high_ref[...], low_ref[...]])
    products = ([], [], [])
    for plane in range(planes):
        a_re, a_im = averages[0, 0, plane], averages[0, 1, plane]
        b_re, b_im = averages[1, 0, plane], averages[1, 1, plane]
        products[0].append(a_re * b_re + a_im * b_im)
        products[1].append(a_re * a_re + a_im * a_im)
        products[2].append(b_re * b_re + b_im * b_im)
    parts = split(jnp.concatenate(products[0] + products[1] + products[2], axis=0))
    by_row = matmul(jnp.concatenate(parts, axis=0), member_ref[...], ((1,), (1,)))
    count = by_row.shape[0] // 2
    by_row = by_row[:count] + by_row[count:]
    by_row = by_row * block_ref[...]
    row_lane = iota((1, LANES), 1)
    shell_sums = jnp.zeros((1, LANES), jnp.float32)
    for which in range(3):
        block = by_row[which * planes * rows : (which + 1) * planes * rows]
        folded = sum(
            block[plane * rows : (plane + 1) * rows, start : start + LANES]
            for plane in range(planes)
            for start in range(0, by_row.shape[1], LANES)
        )
        folded = jnp.sum(folded, axis=0, keepdims=True)
        shift = LANES // 2
        while shift >= NSHELL:
            folded = folded + pltpu.roll(folded, shift, 1)
            shift //= 2
        shell_sums = jnp.where(row_lane // NSHELL == which, folded, shell_sums)
    out_ref[pl.ds(out_stride - 1, devices, stride=out_stride), :] = jnp.broadcast_to(
        shell_sums, (devices, LANES)
    )

    offset = len(order) * rows
    blocks = {}
    for number, (half, plane) in enumerate(order):
        real = back[number * rows : (number + 1) * rows]
        imag = back[offset + number * rows : offset + (number + 1) * rows]
        blocks[half, 0, plane] = real[:, :extent] - imag[:, extent:]
        blocks[half, 1, plane] = real[:, extent:] + imag[:, :extent]
    sequence = [
        blocks[half, part, plane]
        for half in range(2)
        for part in range(2)
        for plane in range(planes)
    ]
    lane = iota((rows, LANES), 1)
    straight = lane // (LANES // 2) == iota((rows, LANES), 0) // (rows // 2)
    group_size = LANES // rows
    for group in range(extent // LANES):
        tiles = [block[:, group * LANES : (group + 1) * LANES] for block in sequence]
        distance = 1
        while distance < len(tiles):
            shift = distance * rows
            clear = (lane & shift) == 0
            for low in range(len(tiles)):
                if low & distance:
                    continue
                high = low | distance
                a, b = tiles[low], tiles[high]
                tiles[low] = jnp.where(clear, a, pltpu.roll(b, shift, 1))
                tiles[high] = jnp.where(clear, pltpu.roll(a, LANES - shift, 1), b)
            distance *= 2
        for number, tile in enumerate(tiles):
            crossed = pltpu.roll(pltpu.roll(tile, LANES // 2, 1), rows // 2, 0)
            packed = jnp.where(straight, tile, crossed)
            for upper in range(2):
                device = group * group_size + upper * (group_size // 2) + number
                start = device * out_stride
                out_ref[start : start + rows // 2, :] = packed[
                    upper * (rows // 2) : (upper + 1) * (rows // 2)
                ]


def finish_kernel(rows, arrived_ref, high_ref, low_ref, maps_ref, fsc_ref):
    halves, parts, planes, own, extent = maps_ref.shape
    devices = extent // rows
    stride = arrived_ref.shape[0] // devices
    total = jnp.sum(
        arrived_ref[pl.ds(stride - 1, devices, stride=stride), :], axis=0, keepdims=True
    )
    cross = total[:, :NSHELL]
    power = total[:, NSHELL : 2 * NSHELL] * total[:, 2 * NSHELL : 3 * NSHELL]
    fsc_ref[...] = cross / (jnp.sqrt(power) + 1e-06)

    gathered = jnp.concatenate(
        [arrived_ref[pl.ds(row, devices, stride=stride), :] for row in range(rows // 2)], axis=0
    )
    turned = gathered.T
    left = jnp.concatenate([turned[: LANES // 2], turned[LANES // 2 :]], axis=1)
    final = matmul_rows(split(left), [high_ref[...], low_ref[...]])
    for half in range(halves):
        for plane in range(planes):
            real_at = ((half * parts + 0) * planes + plane) * own
            imag_at = ((half * parts + 1) * planes + plane) * own
            real = final[real_at : real_at + own]
            imag = final[imag_at : imag_at + own]
            maps_ref[half, 0, plane] = real[:, :extent] - imag[:, extent:]
            maps_ref[half, 1, plane] = real[:, extent:] + imag[:, :extent]


small_grant = pltpu.CompilerParams(vmem_limit_bytes=16 * 1024 * 1024)


def in_vmem(count):
    return [pl.BlockSpec(memory_space=pltpu.VMEM)] * count


def exchange(values, devices):
    chunks = values.reshape(devices, values.shape[0] // devices, 1, LANES)
    return lax.all_to_all(chunks, axes, 0, 0, tiled=True).reshape(values.shape)


def fits(particles, shell_map, devices):
    rows = shell_map.shape[1]
    planes = particles.shape[2]
    extent = shell_map.shape[2]
    return (
        particles.shape[0] == 1
        and rows == SUBLANES
        and rows * devices == extent
        and particles.shape[3] == LANES
        and extent % LANES == 0
        and 4 * planes * rows * 2 == LANES
        and ROW_LANE + 2 * planes * rows <= LANES
        and extent * 2 >= LANES
    )


def shards(particles, orientation, wedge_index, half_set, shell_map):
    devices = lax.axis_size("px") * lax.axis_size("py")
    if not fits(particles, shell_map, devices):
        return general(particles, orientation, wedge_index, half_set, shell_map)
    planes = particles.shape[2]
    box_side = particles.shape[3]
    rows = shell_map.shape[1]
    extent = shell_map.shape[2]
    spectral = np.arange(extent)

    along_x = np.concatenate(
        cos_sin(spectral, np.arange(box_side) - box_side // 2, extent), axis=1
    )
    x_table = np.concatenate(split_table(along_x), axis=1)
    full = np.concatenate(cos_sin(spectral, spectral, extent), axis=1)
    y_high, y_low = split_table(full)
    half_rows = rows // 2
    arrival = (
        np.arange(2)[:, None, None] * half_rows
        + np.arange(half_rows)[None, :, None]
        + np.arange(devices)[None, None, :] * rows
    ).reshape(-1)
    back_high, back_low = split_table(full[arrival])

    smem = pl.BlockSpec(memory_space=pltpu.SMEM)
    labels = pl.pallas_call(
        functools.partial(label_kernel, rows, planes, extent),
        out_shape=jax.ShapeDtypeStruct((devices, LANES), jnp.float32),
        in_specs=[smem] * 3,
        out_specs=in_vmem(1)[0],
        compiler_params=small_grant,
        cost_estimate=pl.CostEstimate(flops=140000000, bytes_accessed=0, transcendentals=0),
    )(orientation, wedge_index, half_set)
    sent = pl.pallas_call(
        functools.partial(spread_kernel, rows),
        out_shape=jax.ShapeDtypeStruct((devices * (2 * planes * rows + 1), LANES), jnp.float32),
        in_specs=[smem] * 2 + in_vmem(3),
        out_specs=in_vmem(1)[0],
        compiler_params=small_grant,
    )(orientation, wedge_index, particles, x_table, labels)
    arrived = exchange(sent, devices)
    middle = pl.pallas_call(
        functools.partial(average_kernel, rows, planes),
        out_shape=jax.ShapeDtypeStruct((devices * (half_rows + 1), LANES), jnp.float32),
        in_specs=in_vmem(4),
        out_specs=in_vmem(1)[0],
        scratch_shapes=[
            pltpu.VMEM((planes * rows * NSHELL, extent), jnp.bfloat16),
            pltpu.VMEM((devices, extent), jnp.bfloat16),
            pltpu.VMEM((3 * planes * rows, planes * rows * NSHELL), jnp.float32),
        ],
        compiler_params=small_grant,
    )(arrived, shell_map, y_high, y_low)
    returned = exchange(middle, devices)
    half_maps, fsc = pl.pallas_call(
        functools.partial(finish_kernel, rows),
        out_shape=(
            jax.ShapeDtypeStruct((2, 2, planes, rows, extent), jnp.float32),
            jax.ShapeDtypeStruct((1, NSHELL), jnp.float32),
        ),
        in_specs=in_vmem(3),
        out_specs=tuple(in_vmem(2)),
        compiler_params=small_grant,
    )(returned, back_high, back_low)
    return half_maps, fsc.reshape(NSHELL)


def select(lookup, position):
    entries = jnp.array(lookup)
    return jnp.sum(jnp.where(jnp.arange(len(lookup)) == position, entries, jnp.zeros_like(entries)))


def angle_table(sources, targets, extent):
    phases = sources[:, None] * targets[None, :] % extent
    angles = phases.astype(jnp.float32) * (2.0 * math.pi / extent)
    factor = 1.0 / math.sqrt(extent)
    return (jnp.cos(angles) * factor, jnp.sin(angles) * factor)


def coverage(plane_abs, spectral_abs, wedge_id):
    rise_value = select(wedge_rise, wedge_id)
    run_value = select(wedge_run, wedge_id)
    return (plane_abs[:, None] * run_value <= spectral_abs[None, :] * rise_value).astype(
        jnp.float32
    )


def general(particles, orientation, wedge_index, half_set, shell_map):
    planes = particles.shape[2]
    box_side = particles.shape[3]
    extent = shell_map.shape[2]
    own_rows = shell_map.shape[1]
    plane_abs = jnp.abs((jnp.arange(planes, dtype=jnp.int32) - planes // 2) * (extent // planes))
    spectral = jnp.arange(extent, dtype=jnp.int32)
    spectral_abs = jnp.minimum(spectral, extent - spectral)
    cos_fwd, sin_fwd = angle_table(
        jnp.arange(box_side, dtype=jnp.int32) - box_side // 2, spectral, extent
    )
    totals = jnp.zeros((2, 2, planes, extent, extent), jnp.float32)
    source = particles[0]
    turn_index = orientation[0]
    swapped = turn_index % 2 == 1
    source = jnp.where(turn_index >= 4, jnp.roll(jnp.flip(source, 1), 1, 1), source)
    source = jnp.where(swapped, jnp.swapaxes(source, 2, 3), source)
    sign_outer = select(sign_first, turn_index)
    sign_inner = select(sign_second, turn_index)
    along_cos = jnp.einsum("czab,bk->czak", source, cos_fwd, precision=highest)
    along_sin = jnp.einsum("czab,bk->czak", source, sin_fwd, precision=highest)
    partial_turn = jnp.stack(
        [along_cos[0] + sign_inner * along_sin[1], along_cos[1] - sign_inner * along_sin[0]]
    )
    outer_cos = jnp.einsum("czak,aj->czjk", partial_turn, cos_fwd, precision=highest)
    outer_sin = jnp.einsum("czak,aj->czjk", partial_turn, sin_fwd, precision=highest)
    spectrum = jnp.stack(
        [outer_cos[0] + sign_outer * outer_sin[1], outer_cos[1] - sign_outer * outer_sin[0]]
    )
    covered = coverage(plane_abs, spectral_abs, wedge_index[0])
    covered = jnp.where(swapped, covered[:, None, :], covered[:, :, None])
    half_id = half_set[0]
    current = lax.dynamic_index_in_dim(totals, half_id, 0, False)
    totals = lax.dynamic_update_index_in_dim(totals, current + spectrum * covered, half_id, 0)
    reduced = lax.psum_scatter(totals, ("px", "py"), scatter_dimension=3, tiled=True)
    half_hot = (half_set[:, None] == jnp.arange(2)).astype(jnp.float32)
    wedge_hot = (wedge_index[:, None] == jnp.arange(4)).astype(jnp.float32)
    parity_hot = (orientation[:, None] % 2 == jnp.arange(2)).astype(jnp.float32)
    local_counts = jnp.einsum("ph,pw,pq->hwq", half_hot, wedge_hot, parity_hot, precision=highest)
    class_totals = lax.psum(local_counts, ("px", "py"))
    row_abs = lax.dynamic_slice_in_dim(
        spectral_abs, lax.axis_index(("px", "py")) * own_rows, own_rows
    )
    row_cover = jnp.stack([coverage(plane_abs, row_abs, wedge_id) for wedge_id in range(4)])
    column_cover = jnp.stack([coverage(plane_abs, spectral_abs, wedge_id) for wedge_id in range(4)])
    by_rows = jnp.einsum("hw,wzt->hzt", class_totals[:, :, 0], row_cover, precision=highest)
    by_columns = jnp.einsum("hw,wzk->hzk", class_totals[:, :, 1], column_cover, precision=highest)
    cover = by_rows[:, :, :, None] + by_columns[:, :, None, :]
    average = reduced / jnp.maximum(cover, 1.0)[:, None]
    cross = average[0, 0] * average[1, 0] + average[0, 1] * average[1, 1]
    power_first = average[0, 0] * average[0, 0] + average[0, 1] * average[0, 1]
    power_second = average[1, 0] * average[1, 0] + average[1, 1] * average[1, 1]
    stacked = jnp.stack([cross, power_first, power_second]).reshape(3, -1)
    membership = (shell_map.reshape(-1)[:, None] == jnp.arange(NSHELL)).astype(jnp.float32)
    shell_part = jnp.dot(stacked, membership, precision=highest)
    shell_total = lax.psum(shell_part, ("px", "py"))
    fsc = shell_total[0] / (jnp.sqrt(shell_total[1] * shell_total[2]) + 1e-06)
    n_rows = lax.axis_size("px")
    n_columns = lax.axis_size("py")
    cos_y, sin_y = angle_table(spectral, spectral, extent)
    middle_cos = jnp.einsum("hcztk,kp->hczpt", average, cos_y, precision=highest)
    middle_sin = jnp.einsum("hcztk,kp->hczpt", average, sin_y, precision=highest)
    middle = jnp.stack(
        [middle_cos[:, 0] - middle_sin[:, 1], middle_sin[:, 0] + middle_cos[:, 1]], axis=1
    )
    arrived = lax.all_to_all(
        lax.all_to_all(middle, "px", split_axis=3, concat_axis=4, tiled=True),
        "py",
        split_axis=3,
        concat_axis=4,
        tiled=True,
    )
    x_slot = spectral // own_rows
    x_source = (x_slot % n_rows * n_columns + x_slot // n_rows) * own_rows + spectral % own_rows
    cos_x, sin_x = angle_table(x_source, spectral, extent)
    final_cos = jnp.einsum("hczym,mx->hczyx", arrived, cos_x, precision=highest)
    final_sin = jnp.einsum("hczym,mx->hczyx", arrived, sin_x, precision=highest)
    half_maps = jnp.stack(
        [final_cos[:, 0] - final_sin[:, 1], final_sin[:, 0] + final_cos[:, 1]], axis=1
    )
    return (half_maps, fsc)


def solution(mesh):
    placed = (
        P(("px", "py"), None, None, None, None),
        P(("px", "py")),
        P(("px", "py")),
        P(("px", "py")),
        P(None, ("px", "py"), None),
    )
    return jax.shard_map(
        shards,
        mesh=mesh,
        in_specs=placed,
        out_specs=(P(None, None, None, ("px", "py"), None), P()),
        check_vma=False,
    )
```
